32 devices in a mesh: nest: 4 (over x, core), py: 2 (over y), px: 4 (over z).
Axes of the slice: x: 2, y: 2, z: 4, core: 2. Of those that a mesh axis runs over, the one named last changes fastest.
Arguments:
- initial_state: float32 [4, 4, 256, 256], P('nest', None, 'px', 'py'), may hold values from -6 to 6
- drive_modes: float32 [3, 4, 64, 64], replicated, may hold values from -6 to 6
- relax_rates: float32 [4, 4], P('nest'), may hold values from 0.2 to 0.9
- nest_offsets: int32 [4, 2], replicated, may hold values from 0 to 170
Outputs:
- final_state: float32 [4, 4, 256, 256], P('nest', None, 'px', 'py')
- final_modes: float32 [4, 4, 64, 64], P('nest')
The draws below stay inside these ranges and needn't reach their ends.
Inputs may be any that keep to these rules, and one draw needn't show every extreme that they name: `nest_offsets`: row 0 is not read.
All inputs are finite; a program needn't handle non-finite values.
Results may differ from the reference program's by a relative error of at most 0.0001.
Values sent between devices are 32-bit elements; how exact they have to be, the bound alone decides.
A program may use at most 64 MiB of HBM per device.

```python
import math
import jax
import jax.numpy as jnp
from jax import lax

LEV = 4
M = 64
RATIO = 3
WIN = 3
NX = 256
NY = 256
N_NEST = 4


def touch_ends(array, stream_key, smallest, high):
    place = [jax.random.randint(jax.random.fold_in(stream_key, axis), (), 0, length) for axis, length in enumerate(array.shape)]
    longest = array.shape.index(max(array.shape))
    next_to = place[:longest] + [(place[longest] + 1) % array.shape[longest]] + place[longest + 1:]
    return array.at[tuple(place)].set(smallest).at[tuple(next_to)].set(high)


def block_scale(rng, shape, split, least, largest):
    loudness = 1.0
    for dim, parts in split:
        heights = jax.random.uniform(jax.random.fold_in(jax.random.fold_in(rng, 6), dim), (parts,), jnp.float32, least / len(split), largest / len(split))
        loudness = loudness * jnp.repeat(jnp.exp(heights), shape[dim] // parts).reshape((-1,) + (1,) * (len(shape) - 1 - dim))
    return loudness


def bell_draw(key, shape, scale, most, split=(), kind=jnp.bfloat16):
    entries = scale * jax.random.normal(key, shape, jnp.float32)
    if split:
        entries = entries * block_scale(key, shape, split, -0.22, 0.18)
    return jnp.clip(entries, -most, most).astype(kind)


def setup_inputs(seed: int = 0) -> dict:
    splits = jax.random.split(jax.random.key(seed), 5)
    return {
        "initial_state": bell_draw(splits[0], (N_NEST, LEV, NX, NY), 1.0, 6.0, ((0, 4), (2, 4), (3, 2)), jnp.float32),
        "drive_modes": bell_draw(splits[1], (WIN, LEV, M, M), 1.0, 6.0, (), jnp.float32),
        "relax_rates": jnp.clip(jnp.exp(math.log(0.9) - 1.50407736 * jax.random.uniform(splits[2], (N_NEST, LEV), jnp.float32) ** block_scale(splits[2], (N_NEST, LEV), ((0, 4),), -0.2, 0.2)), 0.2, 0.9),
        "nest_offsets": touch_ends(jax.random.randint(splits[3], (N_NEST, 2), 0, min(NX, NY) - min(NX, NY) // RATIO), jax.random.fold_in(splits[3], 1), 0, (min(NX, NY) - min(NX, NY) // RATIO) - 1).astype(jnp.int32),
    }


highest = lax.Precision.HIGHEST
diffusion_rate = 0.2

def cosine_basis(numerator, cell_count, mode_count, refine):
    wavenum = jnp.arange(mode_count, dtype=jnp.int32)
    product = wavenum[None, :] * numerator[:, None] % (4 * refine * cell_count)
    angles = jnp.pi * product.astype(jnp.float32) / (2.0 * refine * cell_count)
    weight = jnp.where(wavenum == 0, 1.0, 2.0).astype(jnp.float32) / cell_count
    return jnp.sqrt(weight)[None, :] * jnp.cos(angles)

def diffuse(field_now):
    padded = jnp.pad(field_now, ((0, 0), (1, 1), (1, 1)))
    beside_all = padded[:, 2:, 1:-1] + padded[:, :-2, 1:-1] + padded[:, 1:-1, 2:] + padded[:, 1:-1, :-2]
    return field_now + diffusion_rate * (beside_all - 4.0 * field_now)

def reference(initial_state, drive_modes, relax_rates, nest_offsets):
    cells_x = jnp.arange(NX, dtype=jnp.int32)
    cells_y = jnp.arange(NY, dtype=jnp.int32)
    row_basis = cosine_basis(2 * cells_x + 1, NX, M, 1)
    col_basis = cosine_basis(2 * cells_y + 1, NY, M, 1)
    interp_maps = []
    for domain in range(N_NEST):
        shifted_x = cosine_basis(2 * RATIO * nest_offsets[domain, 0] + 2 * cells_x + 1, NX, M, RATIO)
        shifted_y = cosine_basis(2 * RATIO * nest_offsets[domain, 1] + 2 * cells_y + 1, NY, M, RATIO)
        interp_maps.append((jnp.dot(row_basis.T, shifted_x, precision=highest), jnp.dot(col_basis.T, shifted_y, precision=highest)))
    fields = [initial_state[domain] for domain in range(N_NEST)]
    coeffs = [None] * N_NEST
    for window in range(WIN):
        for domain in range(N_NEST):
            stepped = diffuse(fields[domain])
            partial_rows = jnp.einsum('lxy,ym->lxm', stepped, col_basis, precision=highest)
            own = jnp.einsum('xj,lxm->ljm', row_basis, partial_rows, precision=highest)
            if domain == 0:
                target = drive_modes[window]
            else:
                row_map, col_map = interp_maps[domain]
                target = jnp.einsum('jp,lpq,mq->ljm', row_map, coeffs[domain - 1], col_map, precision=highest)
            change = relax_rates[domain][:, None, None] * (target - own)
            coeffs[domain] = own + change
            back_rows = jnp.einsum('ljm,ym->ljy', change, col_basis, precision=highest)
            fields[domain] = stepped + jnp.einsum('xj,ljy->lxy', row_basis, back_rows, precision=highest)
    return (jnp.stack(fields), jnp.stack(coeffs))
```

```python
import math

import jax
import jax.numpy as jnp
import numpy as np
from jax import lax
from jax.sharding import PartitionSpec as P

RATIO = 3
RATE = 0.2
HI = lax.Precision.HIGHEST


def basis(cells, modes, refine, fn=np.cos):
    j = np.arange(modes, dtype=np.int64)
    q = 2 * np.arange(cells, dtype=np.int64) + 1
    product = (j[None, :] * q[:, None]) % (4 * refine * cells)
    weight = np.where(j == 0, 1.0, 2.0) / cells
    return np.sqrt(weight)[None, :] * fn(np.pi * product / (2.0 * refine * cells))


def half_step(table):
    pad = np.pad(table, ((1, 1), (0, 0)))
    return (0.5 - 2 * RATE) * table + RATE * (pad[2:] + pad[:-2])


def powers(table, count):
    out = [table]
    for _ in range(count):
        out.append(half_step(out[-1]))
    return out


def offset_map(cells, modes, offset):
    base = basis(cells, modes, 1)
    even = jnp.asarray(base.T @ basis(cells, modes, RATIO), jnp.float32)
    odd = jnp.asarray(base.T @ basis(cells, modes, RATIO, np.sin), jnp.float32)
    j = jnp.arange(modes, dtype=jnp.int32)
    product = (j * (2 * RATIO * offset)) % (4 * RATIO * cells)
    angle = jnp.pi * product.astype(jnp.float32) / (2.0 * RATIO * cells)
    return even * jnp.cos(angle)[None, :] - odd * jnp.sin(angle)[None, :]


def exchange(value, axis, dim, width):
    n, length = lax.axis_size(axis), value.shape[dim]
    up = [(i, i + 1) for i in range(n - 1)]
    down = [(i + 1, i) for i in range(n - 1)]
    before = lax.ppermute(lax.slice_in_dim(value, length - width, length, axis=dim), axis, up)
    after = lax.ppermute(lax.slice_in_dim(value, 0, width, axis=dim), axis, down)
    return jnp.concatenate([before, value, after], axis=dim)


def free_steps(field, total_x, total_y, steps):
    levels, cx, cy = field.shape
    pad = exchange(exchange(field, "py", 2, steps), "px", 1, steps)
    gx = lax.axis_index("px") * cx - steps + jnp.arange(cx + 2 * steps)
    gy = lax.axis_index("py") * cy - steps + jnp.arange(cy + 2 * steps)
    inside = ((gx >= 0) & (gx < total_x))[:, None] & ((gy >= 0) & (gy < total_y))[None, :]
    for s in range(steps):
        mid = pad[:, 1:-1, 1:-1]
        near = pad[:, 2:, 1:-1] + pad[:, :-2, 1:-1] + pad[:, 1:-1, 2:] + pad[:, 1:-1, :-2]
        pad = mid + RATE * (near - 4.0 * mid)
        cut = s + 1
        pad = jnp.where(inside[cut:-cut, cut:-cut][None], pad, 0.0)
    return pad


def body(initial_state, drive_modes, relax_rates, nest_offsets):
    k = lax.axis_index("nest")
    nests = lax.axis_size("nest")
    field = initial_state[0]
    levels, cx, cy = field.shape
    windows, _, m, _ = drive_modes.shape
    nx, ny = cx * lax.axis_size("px"), cy * lax.axis_size("py")
    rp, cp = powers(basis(nx, m, 1), windows), powers(basis(ny, m, 1), windows)
    a = [jnp.asarray(rp[0].T @ t, jnp.float32) for t in rp]
    b = [jnp.asarray(cp[0].T @ t, jnp.float32) for t in cp]
    u_all = jnp.asarray(np.concatenate(rp, 1), jnp.float32)
    v_all = jnp.asarray(np.concatenate(cp, 1), jnp.float32)
    u = lax.dynamic_slice_in_dim(u_all, lax.axis_index("px") * cx, cx, 0)
    v = lax.dynamic_slice_in_dim(v_all, lax.axis_index("py") * cy, cy, 0)

    half = jnp.einsum("lxy,yq->lxq", field, v, precision=HI)
    rows = []
    for w in range(1, windows + 1):
        terms = [math.comb(w, i) * half[:, :, (w - i) * m : (w - i + 1) * m] for i in range(w + 1)]
        rows.append(
            jnp.einsum(
                "xj,lxm->ljm",
                jnp.concatenate([u[:, i * m : (i + 1) * m] for i in range(w + 1)], 0),
                jnp.concatenate(terms, 1),
                precision=HI,
            )
        )
    shares = lax.psum(jnp.stack(rows), ("py", "px"))

    gain = relax_rates[0][:, None, None]
    row_map = offset_map(nx, m, nest_offsets[k, 0])
    col_map = offset_map(ny, m, nest_offsets[k, 1])

    def left(t, x):
        return jnp.einsum("jp,lpq->ljq", t, x, precision=HI)

    def right(x, t):
        return jnp.einsum("ljq,mq->ljm", x, t, precision=HI)

    def spread(d, x):
        out = left(a[d], x) + right(x, b[d])
        for i in range(1, d):
            out = out + math.comb(d, i) * right(left(a[i], x), b[d - i])
        return out

    parent = jnp.zeros_like(drive_modes)
    for stage in range(nests):
        if stage:
            parent = lax.ppermute(coeffs, "nest", [(i, i + 1) for i in range(nests - 1)])
            interp = jnp.einsum("jp,wlpq->wljq", row_map, parent, precision=HI)
            interp = jnp.einsum("wljq,mq->wljm", interp, col_map, precision=HI)
            target = jnp.where(k == 0, drive_modes, interp)
        else:
            target = drive_modes
        changes, kept = [], []
        for w in range(windows):
            own = shares[w]
            for e in range(w):
                own = own + spread(w - e, changes[e])
            changes.append(gain * (target[w] - own))
            kept.append(own + changes[-1])
        coeffs = jnp.stack(kept)

    free = free_steps(field, nx, ny, windows)
    zero = jnp.zeros_like(changes[0])
    blocks = [
        jnp.concatenate(
            [
                math.comb(i + j, i) * changes[windows - 1 - i - j] if i + j < windows else zero
                for j in range(windows)
            ],
            2,
        )
        for i in range(windows)
    ]
    mixed = jnp.concatenate(blocks, 1)
    wide = windows * m
    back = jnp.einsum("lpq,yq->lpy", mixed, v[:, :wide], precision=HI)
    final = free + jnp.einsum("xp,lpy->lxy", u[:, :wide], back, precision=HI)
    return final[None], coeffs[windows - 1][None]


def solution(mesh):
    spec = P("nest", None, "px", "py")
    return jax.shard_map(
        body,
        mesh=mesh,
        in_specs=(spec, P(), P("nest", None), P()),
        out_specs=(spec, P("nest", None, None, None)),
        check_vma=False,
    )
```
